256 devices in a mesh: obl: 8 (over z_hi, x), scen: 32 (over y, z_lo, core).
Axes of the slice: x: 4, y: 4, z: 8 (z_hi: 2, z_lo: 4; z = z_hi * 4 + z_lo), core: 2. Of those that a mesh axis runs over, the one named last changes fastest.
Arguments:
- loadings: bfloat16 [32768, 256], P('obl', 'scen'), may hold values from -0.375 to 0.375
- scenarios: bfloat16 [256, 131072], P('obl', 'scen'), may hold values from -6 to 6
- rho: float32 [32768], P('obl'), may hold values from 0.05 to 0.5
- exposure: float32 [32768], P('obl'), may hold values from 0.5 to 20
- rating: int32 [32768], P('obl'), may hold values from 0 to 15
- thresholds: float32 [16], replicated, may hold values from -3 to -1
- tail_weight: int32 [131072], P('scen'), may hold values from 1 to 8, as said below
Outputs:
- losses: float32 [131072], P('scen')
- contributions: float32 [32768], P('obl')
- shortfall: float32 [], replicated
The draws below stay inside these ranges and needn't reach their ends.
Inputs may be any that keep to these rules, and one draw needn't show every extreme that they name: `tail_weight`: weights are larger on average toward later scenarios.
All inputs are finite; a program needn't handle non-finite values.
Results may differ from the reference program's by a relative error of at most 0.0003.
Values may be sent and summed in bfloat16 or wider, within the bound.
A program may use at most 256 MiB of HBM per device.

```python
import math
import jax
import jax.numpy as jnp
from jax import lax

F = 256
RATINGS = 16
NOBL = 32768
NSC = 131072


def draw_tail_weight(key, part):
    position = jnp.arange(NSC).astype(jnp.int32)
    upper = 3 + 7 * position // NSC
    return jax.random.randint(key, (NSC,), 1, upper).astype(jnp.int32)


def plant(result, stream_key, low, top_value):
    longest = result.shape.index(max(result.shape))
    spots = []
    for shift in (0, 1):
        where = [jax.random.randint(jax.random.fold_in(stream_key, axis), (), 0, length) for axis, length in enumerate(result.shape)]
        where[longest] = (where[longest] + shift) % result.shape[longest]
        spots.append(tuple(where))
    return result.at[spots[0]].set(low).at[spots[1]].set(top_value)


def block_levels(own_key, dims, cuts, smallest, high):
    gain, own = 1.0, jax.random.fold_in(own_key, 6)
    for dim, shards_of in cuts:
        steps = jnp.exp(jax.random.uniform(jax.random.fold_in(own, dim), (shards_of,), jnp.float32, smallest / len(cuts), high / len(cuts)))
        gain = gain * jnp.repeat(steps, dims[dim] // shards_of).reshape([-1 if axis == dim else 1 for axis in range(len(dims))])
    return gain


def normal_values(stream_key, dims, deviation, limit, shards=(), dtype=jnp.bfloat16):
    array = jax.random.normal(stream_key, dims, jnp.float32) * deviation
    if len(shards) > 0:
        array = block_levels(stream_key, dims, shards, -0.22, 0.18) * array
    return jnp.clip(array, min=-limit, max=limit).astype(dtype)


def setup_inputs(seed: int = 0) -> dict:
    streams_of = jax.random.split(jax.random.key(seed), 8)
    return {
        "loadings": normal_values(streams_of[0], (NOBL, F), F ** -0.5, 0.375, ((0, 8), (1, 32))),
        "scenarios": normal_values(streams_of[1], (F, NSC), 1.0, 6.0, ((0, 8), (1, 32))),
        "rho": jnp.clip(jnp.exp(math.log(0.5) - 2.3025851 * jax.random.uniform(streams_of[2], (NOBL,), jnp.float32) ** block_levels(streams_of[2], (NOBL,), ((0, 8),), -0.2, 0.2)), 0.05, 0.5),
        "exposure": jnp.clip(jnp.exp(math.log(20.0) - 3.6888795 * jax.random.uniform(streams_of[3], (NOBL,), jnp.float32) ** block_levels(streams_of[3], (NOBL,), ((0, 8),), -0.2, 0.2)), 0.5, 20.0),
        "rating": plant(jax.random.randint(streams_of[4], (NOBL,), 0, RATINGS), jax.random.fold_in(streams_of[4], 1), 0, RATINGS - 1).astype(jnp.int32),
        "thresholds": jnp.clip(jax.random.uniform(streams_of[5], (RATINGS,), jnp.float32, -3.0, -1.0), -3.0, -1.0),
        "tail_weight": draw_tail_weight(jax.random.fold_in(streams_of[7], 71), 0),
    }


def normal_cdf(value):
    return 0.5 * lax.erfc(-value * 0.7071067811865476)

def reference(loadings, scenarios, rho, exposure, rating, thresholds, tail_weight):
    loads = loadings.astype(jnp.float32)
    sumsq = lax.optimization_barrier(jnp.sum(loads * loads, axis=1))
    scale = lax.rsqrt(sumsq + 1e-06)
    buckets = jnp.arange(RATINGS).astype(jnp.int32)
    thr = lax.optimization_barrier(jnp.sum(jnp.where(rating[:, None] == buckets[None, :], thresholds[None, :], jnp.float32(0.0)), axis=1))
    root_rho = jnp.sqrt(rho)
    root_rest = jnp.sqrt(1.0 - rho)
    count = loadings.shape[0]
    width = math.gcd(NSC, 512)
    nblocks = NSC // width
    blocks = jnp.transpose(scenarios.reshape(F, nblocks, width), (1, 0, 2))
    weights = tail_weight.astype(jnp.float32)
    wblocks = weights.reshape(nblocks, width)

    def one_block(pair):
        panel, wpart = pair
        product = jnp.dot(loads, panel.astype(jnp.float32), precision=lax.Precision.HIGHEST, preferred_element_type=jnp.float32)
        systematic = product * scale[:, None]
        pdef = normal_cdf((thr[:, None] - root_rho[:, None] * systematic) / root_rest[:, None])
        weighted = exposure[:, None] * pdef
        return (lax.optimization_barrier(jnp.sum(weighted, axis=0)) / count, lax.optimization_barrier(jnp.sum(weighted * wpart[None, :], axis=1)))
    loss_blocks, numers = lax.map(one_block, (blocks, wblocks))
    losses = loss_blocks.reshape(-1)
    total = jnp.sum(weights)
    contributions = lax.optimization_barrier(jnp.sum(numers, axis=0)) / total
    shortfall = jnp.sum(weights * losses) / total
    return (losses, contributions, shortfall)
```

```python
import functools

import jax
import jax.numpy as jnp
import numpy as np
from jax import lax
from jax.experimental import pallas as pl
from jax.experimental.pallas import tpu as pltpu
from jax.sharding import PartitionSpec as P

LANES = 128
ROWS = 256
COLS = 512

SCALE = float(2.0**-3.4)
OFFSET = float(5.2 * 2.0**-3.4)
COEFFS = (
    -24.48703166417573,
    -58.39165125696405,
    -57.73044940308441,
    -31.529938430810628,
    -11.50559434722367,
    -3.36061823149743,
    -0.771910203459282,
    -0.15406865262823627,
    -0.033933149049334255,
)


def scenario_losses(
    thresholds, lt_ref, s_ref, rho, exposure, rating, weight, loss_out, cont_out,
    st, wide_weight, loss, cont, shift, slope, expo, base, prod_a, prod_b,
):
    factors, nobl = lt_ref.shape
    nsc = s_ref.shape[1]

    for r in range(nobl // LANES):
        block = lt_ref[:, r * LANES : (r + 1) * LANES].astype(jnp.float32)
        slope[r : r + 1, :] = jnp.sum(block * block, axis=0, keepdims=True)
    kind = rating[...]
    thr = jnp.zeros(kind.shape, jnp.float32)
    for k in range(thresholds.shape[0]):
        thr = jnp.where(kind == k, thresholds[k], thr)
    root_rest = jnp.sqrt(1.0 - rho[...])
    scale = lax.rsqrt(slope[...] + 1e-06)
    shift[...] = thr / root_rest * SCALE
    slope[...] = -(jnp.sqrt(rho[...]) * scale / root_rest) * SCALE
    expo[...] = exposure[...]
    base[...] = jnp.log2(exposure[...]) + COEFFS[0]

    @pl.loop(0, nsc // LANES)
    def _(r):
        at = pl.ds(pl.multiple_of(r * LANES, LANES), LANES)
        st[at, :] = s_ref[:, at].T
        row = weight[pl.ds(r, 1), :].astype(jnp.float32)
        wide_weight[at, :] = jnp.broadcast_to(row, (LANES, LANES)).T

    loss[...] = jnp.zeros_like(loss)
    cont[...] = jnp.zeros_like(cont)
    per = nsc // ROWS
    steps = per * (nobl // COLS)

    def product(step, into):
        jb, ib = step // per, step % per
        rows = pl.ds(pl.multiple_of(ib * ROWS, ROWS), ROWS)
        cols = pl.ds(pl.multiple_of(jb * COLS, COLS), COLS)
        into[...] = jnp.dot(st[rows, :], lt_ref[:, cols], preferred_element_type=jnp.float32)

    tiles = COLS // LANES

    def spread(ref, jb):
        return [jnp.broadcast_to(ref[pl.ds(jb * tiles + j, 1), :], (8, LANES)) for j in range(tiles)]

    def reduce_step(step, prod):
        jb, ib = step // per, step % per
        a, b, e, g = spread(shift, jb), spread(slope, jb), spread(expo, jb), spread(base, jb)
        total = [jnp.zeros((8, LANES), jnp.float32) for _ in range(tiles)]
        for r in range(ROWS // 8):
            at = pl.ds(pl.multiple_of(ib * ROWS + r * 8, 8), 8)
            w = wide_weight[at, :]
            partial = None
            for j in range(tiles):
                v = prod[r * 8 : r * 8 + 8, j * LANES : (j + 1) * LANES] * b[j] + a[j]
                y = jnp.log2(jnp.abs(v) + OFFSET)
                q = y * COEFFS[-1] + COEFFS[-2]
                for c in COEFFS[-3:0:-1]:
                    q = q * y + c
                tail = jnp.exp2(q * y + g[j])
                x = jnp.where(v < 0.0, tail, e[j] - tail)
                total[j] = total[j] + x * w
                partial = x if partial is None else partial + x
            loss[at, :] = loss[at, :] + partial
        for j in range(tiles):
            at = pl.ds(pl.multiple_of(jb * COLS + j * LANES, LANES), LANES)
            cont[:, at] = cont[:, at] + total[j]

    product(0, prod_a)

    @pl.loop(0, steps // 2)
    def _(k):
        product(2 * k + 1, prod_b)
        reduce_step(2 * k, prod_a)
        product(jnp.minimum(2 * k + 2, steps - 1), prod_a)
        reduce_step(2 * k + 1, prod_b)

    for r in range(nsc // LANES):
        loss_out[r : r + 1, :] = jnp.sum(loss[r * LANES : (r + 1) * LANES, :].T, axis=0, keepdims=True)
    for r in range(nobl // LANES):
        cont_out[r : r + 1, :] = jnp.sum(cont[:, r * LANES : (r + 1) * LANES], axis=0, keepdims=True)


def compute(lt, s, rho, exposure, rating, thresholds, weight):
    factors, nobl = lt.shape
    nsc = s.shape[1]
    rows, cols = nobl // LANES, nsc // LANES
    vmem = pl.BlockSpec(memory_space=pltpu.VMEM)
    f32 = jnp.float32
    return pl.pallas_call(
        scenario_losses,
        name="scenario_losses",
        out_shape=(
            jax.ShapeDtypeStruct((cols, LANES), f32),
            jax.ShapeDtypeStruct((rows, LANES), f32),
        ),
        in_specs=[pl.BlockSpec(memory_space=pltpu.SMEM)] + [vmem] * 6,
        out_specs=(vmem, vmem),
        scratch_shapes=[
            pltpu.VMEM((nsc, factors), jnp.bfloat16),
            pltpu.VMEM((nsc, LANES), f32),
            pltpu.VMEM((nsc, LANES), f32),
            pltpu.VMEM((8, nobl), f32),
            pltpu.VMEM((rows, LANES), f32),
            pltpu.VMEM((rows, LANES), f32),
            pltpu.VMEM((rows, LANES), f32),
            pltpu.VMEM((rows, LANES), f32),
            pltpu.VMEM((ROWS, COLS), f32),
            pltpu.VMEM((ROWS, COLS), f32),
        ],
    )(
        thresholds, lt, s, rho.reshape(rows, LANES), exposure.reshape(rows, LANES),
        rating.reshape(rows, LANES), weight.reshape(cols, LANES),
    )


def local(loadings, scenarios, rho, exposure, rating, thresholds, tail_weight):
    panel = lax.all_gather(scenarios, "obl", axis=0, tiled=True)
    lt = lax.all_gather(loadings.T, "scen", axis=0, tiled=True)
    count = loadings.shape[0] * lax.axis_size("obl")
    loss, cont = compute(lt, panel, rho, exposure, rating, thresholds, tail_weight)
    weights = tail_weight.astype(jnp.float32)
    losses = lax.psum(loss.reshape(-1), "obl") / count
    numer, total = lax.psum((cont.reshape(-1), jnp.sum(weights)), "scen")
    contributions = numer / total
    shortfall = lax.psum(jnp.sum(contributions), "obl") / count
    return (losses, contributions, shortfall)


def solution(mesh):
    placed = (P("obl", "scen"), P("obl", "scen"), P("obl"), P("obl"), P("obl"), P(), P("scen"))
    return jax.shard_map(
        local, mesh=mesh, in_specs=placed, out_specs=(P("scen"), P("obl"), P()), check_vma=False
    )
```

```python
import functools

import jax
import jax.numpy as jnp
import numpy as np
from jax import lax
from jax.experimental import pallas as pl
from jax.experimental.pallas import tpu as pltpu
from jax.sharding import PartitionSpec as P

LANES = 128
ROWS = 256
COLS = 512

SCALE = float(2.0**-3.4)
OFFSET = float(5.2 * 2.0**-3.4)
COEFFS = (
    -24.48703166417573,
    -58.39165125696405,
    -57.73044940308441,
    -31.529938430810628,
    -11.50559434722367,
    -3.36061823149743,
    -0.771910203459282,
    -0.15406865262823627,
    -0.033933149049334255,
)


MESH = pl.DeviceIdType.MESH
X, Z, Y, CORES = 4, 4, 4, 2
TILE = 8


def place():
    obl, scen = lax.axis_index("obl"), lax.axis_index("scen")
    return obl // X, obl % X, scen // (Z * CORES), scen // CORES % Z, scen % CORES


def obl_at(far, x):
    return far * X + x


def scen_at(y, z, core):
    return (y * Z + z) * CORES + core


class Links:
    def __init__(self, send_sems):
        self.sems, self.started = send_sems, []

    def send(self, source, target, recv_sem, obl, scen):
        copy = pltpu.make_async_remote_copy(
            src_ref=source, dst_ref=target, send_sem=self.sems.at[len(self.started)],
            recv_sem=recv_sem, device_id={"obl": obl, "scen": scen}, device_id_type=MESH,
        )
        copy.start()
        self.started.append(copy)

    def receive(self, target, recv_sem):
        pltpu.make_async_remote_copy(
            src_ref=target, dst_ref=target, send_sem=self.sems.at[0], recv_sem=recv_sem,
            device_id={"obl": lax.axis_index("obl"), "scen": lax.axis_index("scen")},
            device_id_type=MESH,
        ).wait_recv()

    def finish(self):
        for copy in self.started:
            copy.wait_send()


GATHER_SENDS = 9 + 3 + 16 + 16
REDUCE_SENDS = 2 + 3 + 3 + 3 + 31


def meet(peers):
    barrier = pltpu.get_barrier_semaphore()
    for obl, scen in peers:
        pl.semaphore_signal(
            barrier, inc=1, device_id={"obl": obl, "scen": scen}, device_id_type=MESH)
    pl.semaphore_wait(barrier, len(peers))


def gather(loads, scenarios, lt3, panel, send_sems, local_sem, panel_sem, loads_sem):
    far, x, y, z, core = place()
    obl, scen = lax.axis_index("obl"), lax.axis_index("scen")
    height, nsc = scenarios.shape
    nobl = loads.shape[1]
    half_h, half_w = height // 2, nobl // 2
    right, left = (x + 1) % X, (x + X - 1) % X
    up, down = (y + 1) % Y, (y + Y - 1) % Y
    meet(
        [(obl_at(1 - far, x), scen), (obl_at(far, left), scen), (obl_at(far, right), scen)]
        + [(obl, scen_at(to, z, core)) for to in (up, down)]
        + [(obl, scen_at(y, (z + k) % Z, core)) for k in range(1, Z)]
        + [(obl, scen_at(y, z, 1 - core))]
    )
    links = Links(send_sems)

    def rows(owner, start=0, size=height):
        return panel.at[pl.ds(pl.multiple_of(owner * height + start, half_h), size), :]

    own_rows = pltpu.make_async_copy(scenarios, rows(obl), local_sem.at[0])
    own_loads = pltpu.make_async_copy(loads, lt3.at[scen], local_sem.at[1])
    own_rows.start()
    own_loads.start()

    def panel_out(source, owner):
        for to in (right, left):
            links.send(source, rows(owner), panel_sem.at[owner, 0], obl_at(far, to), scen)

    def panel_relay(row):
        low, high = obl_at(row, left), obl_at(row, right)
        links.receive(rows(low), panel_sem.at[low, 0])
        links.send(
            rows(low, 0, half_h), rows(low, 0, half_h), panel_sem.at[low, 0], obl_at(far, right), scen)
        links.receive(rows(high), panel_sem.at[high, 0])
        links.send(
            rows(high, half_h, half_h), rows(high, half_h, half_h), panel_sem.at[high, 1],
            obl_at(far, left), scen)

    def panel_last(row):
        across = obl_at(row, (x + 2) % X)
        links.receive(rows(across, 0, half_h), panel_sem.at[across, 0])
        links.receive(rows(across, half_h, half_h), panel_sem.at[across, 1])

    def strip(owner, part=None):
        if part is None:
            return lt3.at[owner]
        return lt3.at[owner, :, pl.ds(part * half_w, half_w)]

    def loads_out(source, owner):
        for to in (up, down):
            links.send(source, strip(owner), loads_sem.at[owner, 0], obl, scen_at(to, z, core))
        loads_across(source, owner)

    def loads_across(source, owner):
        links.send(source, strip(owner), loads_sem.at[owner, 0], obl, scen_at(y, z, 1 - core))

    def loads_relay(run):
        low, high = scen_at(down, run, core), scen_at(up, run, core)
        links.receive(strip(low), loads_sem.at[low, 0])
        links.send(strip(low, 0), strip(low, 0), loads_sem.at[low, 0], obl, scen_at(up, z, core))
        loads_across(strip(low), low)
        links.receive(strip(high), loads_sem.at[high, 0])
        links.send(strip(high, 1), strip(high, 1), loads_sem.at[high, 1], obl, scen_at(down, z, core))
        loads_across(strip(high), high)

    def loads_last(run):
        opposite = scen_at((y + 2) % Y, run, core)
        links.receive(strip(opposite, 0), loads_sem.at[opposite, 0])
        links.receive(strip(opposite, 1), loads_sem.at[opposite, 1])
        loads_across(strip(opposite), opposite)

    runs = [(z + k) % Z for k in range(Z)]
    for run in runs[1:]:
        links.send(loads, strip(scen), loads_sem.at[scen, 0], obl, scen_at(y, run, core))
    links.send(scenarios, rows(obl), panel_sem.at[obl, 0], obl_at(1 - far, x), scen)
    panel_out(scenarios, obl)
    loads_out(loads, scen)
    for run in runs[1:]:
        owner = scen_at(y, run, core)
        links.receive(strip(owner), loads_sem.at[owner, 0])
        loads_out(strip(owner), owner)
    loads_relay(runs[0])
    panel_relay(far)
    other = obl_at(1 - far, x)
    links.receive(rows(other), panel_sem.at[other, 0])
    panel_out(rows(other), other)
    for run in runs[1:]:
        loads_relay(run)
    for run in runs:
        loads_last(run)
    panel_relay(1 - far)
    for run in range(Z):
        for k in range(Y):
            owner = scen_at(k, run, 1 - core)
            links.receive(strip(owner), loads_sem.at[owner, 0])
    own_rows.wait()
    own_loads.wait()
    panel_last(far)
    panel_last(1 - far)
    links.finish()


def reduce(
    count, loss_a, cont_a, weight, losses_out, cont_out, short_out,
    loss_z, loss_x, cont_c, cont_z, cont_y, tiles,
    send_sems, sums_sem, loss_sem, run_sem, y_sem, tile_sem,
):
    far, x, y, z, core = place()
    obl, scen = lax.axis_index("obl"), lax.axis_index("scen")
    nrows = losses_out.shape[0]
    group = Y * Z * CORES
    meet(
        [(obl_at(1 - far, x), scen)]
        + [(obl_at(far, (x + k) % X), scen) for k in range(1, X)]
        + [(obl, (scen + k) % group) for k in range(1, group)]
    )
    links = Links(send_sems)
    weights = weight[...].astype(jnp.float32)
    weight_sum = jnp.sum(jnp.sum(weights, axis=0, keepdims=True), axis=1, keepdims=True)

    links.send(loss_a, loss_z, sums_sem.at[0], obl_at(1 - far, x), scen)
    links.send(cont_a, cont_c, sums_sem.at[1], obl, scen_at(y, z, 1 - core))
    links.receive(cont_c, sums_sem.at[1])
    cont_z[z] = cont_a[...] + cont_c[...]
    for k in range(1, Z):
        links.send(cont_z.at[z], cont_z.at[z], run_sem.at[z], obl, scen_at(y, (z + k) % Z, core))
    links.receive(loss_z, sums_sem.at[0])
    loss_x[x] = loss_a[...] + loss_z[...]
    for k in range(1, X):
        links.send(loss_x.at[x], loss_x.at[x], loss_sem.at[x], obl_at(far, (x + k) % X), scen)
    for k in range(1, Z):
        links.receive(cont_z.at[(z + k) % Z], run_sem.at[(z + k) % Z])
    cont_y[y] = cont_z[0] + cont_z[1] + cont_z[2] + cont_z[3]
    for k in range(1, Y):
        links.send(cont_y.at[y], cont_y.at[y], y_sem.at[y], obl, scen_at((y + k) % Y, z, core))
    for k in range(1, X):
        links.receive(loss_x.at[(x + k) % X], loss_sem.at[(x + k) % X])
    whole = loss_x[0] + loss_x[1] + loss_x[2] + loss_x[3]
    losses_out[...] = whole[:nrows] / count
    upper = lax.broadcasted_iota(jnp.int32, (TILE, LANES), 0) < TILE // 2
    tiles[scen] = jnp.where(upper, whole[nrows:], jnp.broadcast_to(weight_sum, (TILE, LANES)))
    for k in range(1, group):
        links.send(tiles.at[scen], tiles.at[scen], tile_sem.at[scen], obl, (scen + k) % group)
    for k in range(1, Y):
        links.receive(cont_y.at[(y + k) % Y], y_sem.at[(y + k) % Y])
    numer = cont_y[0] + cont_y[1] + cont_y[2] + cont_y[3]
    for k in range(1, group):
        links.receive(tiles.at[(scen + k) % group], tile_sem.at[(scen + k) % group])
    scalars = jnp.sum(tiles[...], axis=0)
    total = scalars[TILE - 1 : TILE, :]
    cont_out[...] = numer / total
    short_out[...] = jnp.broadcast_to(scalars[0:1, :] / total / count, (TILE, LANES))
    links.finish()


def scenario_losses(
    thresholds, lt3, panel, rho, exposure, rating, weight, loss_out, cont_out,
    lt, st, wide_weight, loss, cont, shift, slope, expo, base, prod_a, prod_b,
):
    factors, nobl = lt.shape
    nsc = panel.shape[1]

    for r in range(nobl // LANES):
        at = slice(r * LANES, (r + 1) * LANES)
        square = jnp.zeros((TILE, LANES), jnp.float32)
        for k in range(0, factors // TILE, 2):
            one, two = lt3[k, :, at].astype(jnp.float32), lt3[k + 1, :, at].astype(jnp.float32)
            square = square + one * one + two * two
            lt[k * TILE : (k + 2) * TILE, at] = jnp.concatenate([one, two], axis=0).astype(jnp.bfloat16)
        slope[r : r + 1, :] = jnp.sum(square, axis=0, keepdims=True)
    kind = rating[...]
    thr = jnp.zeros(kind.shape, jnp.float32)
    for k in range(thresholds.shape[0]):
        thr = jnp.where(kind == k, thresholds[k], thr)
    root_rest = jnp.sqrt(1.0 - rho[...])
    scale = lax.rsqrt(slope[...] + 1e-06)
    shift[...] = thr / root_rest * SCALE
    slope[...] = -(jnp.sqrt(rho[...]) * scale / root_rest) * SCALE
    expo[...] = exposure[...]
    base[...] = jnp.log2(exposure[...]) + COEFFS[0]

    @pl.loop(0, nsc // LANES)
    def _(r):
        at = pl.ds(pl.multiple_of(r * LANES, LANES), LANES)
        st[at, :] = panel[:, at].T
        row = weight[pl.ds(r, 1), :].astype(jnp.float32)
        wide_weight[at, :] = jnp.broadcast_to(row, (LANES, LANES)).T

    loss[...] = jnp.zeros_like(loss)
    cont[...] = jnp.zeros_like(cont)
    per = nsc // ROWS
    steps = per * (nobl // COLS)

    def product(step, into):
        jb, ib = step // per, step % per
        rows = pl.ds(pl.multiple_of(ib * ROWS, ROWS), ROWS)
        cols = pl.ds(pl.multiple_of(jb * COLS, COLS), COLS)
        into[...] = jnp.dot(st[rows, :], lt[:, cols], preferred_element_type=jnp.float32)

    tiles = COLS // LANES

    def spread(ref, jb):
        return [jnp.broadcast_to(ref[pl.ds(jb * tiles + j, 1), :], (8, LANES)) for j in range(tiles)]

    def reduce_step(step, prod):
        jb, ib = step // per, step % per
        a, b, e, g = spread(shift, jb), spread(slope, jb), spread(expo, jb), spread(base, jb)
        total = [jnp.zeros((8, LANES), jnp.float32) for _ in range(tiles)]
        for r in range(ROWS // 8):
            at = pl.ds(pl.multiple_of(ib * ROWS + r * 8, 8), 8)
            w = wide_weight[at, :]
            partial = None
            for j in range(tiles):
                v = prod[r * 8 : r * 8 + 8, j * LANES : (j + 1) * LANES] * b[j] + a[j]
                y = jnp.log2(jnp.abs(v) + OFFSET)
                q = y * COEFFS[-1] + COEFFS[-2]
                for c in COEFFS[-3:0:-1]:
                    q = q * y + c
                tail = jnp.exp2(q * y + g[j])
                x = jnp.where(v < 0.0, tail, e[j] - tail)
                total[j] = total[j] + x * w
                partial = x if partial is None else partial + x
            loss[at, :] = loss[at, :] + partial
        for j in range(tiles):
            at = pl.ds(pl.multiple_of(jb * COLS + j * LANES, LANES), LANES)
            cont[:, at] = cont[:, at] + total[j]

    product(0, prod_a)

    @pl.loop(0, steps // 2)
    def _(k):
        product(2 * k + 1, prod_b)
        reduce_step(2 * k, prod_a)
        product(jnp.minimum(2 * k + 2, steps - 1), prod_a)
        reduce_step(2 * k + 1, prod_b)

    for r in range(nsc // LANES):
        loss_out[r : r + 1, :] = jnp.sum(loss[r * LANES : (r + 1) * LANES, :].T, axis=0, keepdims=True)
    for r in range(nobl // LANES):
        cont_out[r : r + 1, :] = jnp.sum(cont[:, r * LANES : (r + 1) * LANES], axis=0, keepdims=True)
    numer_here = jnp.sum(jnp.sum(cont_out[...], axis=0, keepdims=True), axis=1, keepdims=True)
    loss_out[nsc // LANES :, :] = jnp.broadcast_to(numer_here, (TILE, LANES))


def local(loadings, scenarios, rho, exposure, rating, thresholds, tail_weight):
    nobl, nsc = loadings.shape[0], scenarios.shape[1]
    far_x, group = lax.axis_size("obl"), lax.axis_size("scen")
    factors = scenarios.shape[0] * far_x
    count = nobl * far_x
    rows, cols = nobl // LANES, nsc // LANES
    vmem = pl.BlockSpec(memory_space=pltpu.VMEM)
    f32, bf16, dma = jnp.float32, jnp.bfloat16, pltpu.SemaphoreType.DMA
    weight = tail_weight.reshape(cols, LANES)

    def wide(*shape):
        return pltpu.VMEM(shape, f32)

    lt3, panel = pl.pallas_call(
        gather,
        name="gather",
        out_shape=(
            jax.ShapeDtypeStruct((group, factors // group, nobl), bf16),
            jax.ShapeDtypeStruct((factors, nsc), bf16),
        ),
        in_specs=[vmem] * 2,
        out_specs=(vmem, vmem),
        scratch_shapes=[dma((GATHER_SENDS,)), dma((2,)), dma((far_x, 2)), dma((group, 2))],
        compiler_params=pltpu.CompilerParams(collective_id=0, has_side_effects=True),
    )(loadings.T, scenarios)
    loss, cont = pl.pallas_call(
        scenario_losses,
        name="scenario_losses",
        out_shape=(
            jax.ShapeDtypeStruct((cols + TILE, LANES), f32),
            jax.ShapeDtypeStruct((rows, LANES), f32),
        ),
        in_specs=[pl.BlockSpec(memory_space=pltpu.SMEM)] + [vmem] * 6,
        out_specs=(vmem, vmem),
        scratch_shapes=[
            pltpu.VMEM((factors, nobl), bf16),
            pltpu.VMEM((nsc, factors), bf16),
            wide(nsc, LANES), wide(nsc, LANES), wide(8, nobl),
            wide(rows, LANES), wide(rows, LANES), wide(rows, LANES), wide(rows, LANES),
            wide(ROWS, COLS), wide(ROWS, COLS),
        ],
    )(
        thresholds, lt3, panel, rho.reshape(rows, LANES), exposure.reshape(rows, LANES),
        rating.reshape(rows, LANES), weight,
    )
    losses, contributions, shortfall = pl.pallas_call(
        functools.partial(reduce, count),
        name="reduce",
        out_shape=(
            jax.ShapeDtypeStruct((cols, LANES), f32),
            jax.ShapeDtypeStruct((rows, LANES), f32),
            jax.ShapeDtypeStruct((TILE, LANES), f32),
        ),
        in_specs=[vmem] * 3,
        out_specs=(vmem, vmem, vmem),
        scratch_shapes=[
            wide(cols + TILE, LANES), wide(X, cols + TILE, LANES),
            wide(rows, LANES), wide(Z, rows, LANES), wide(Y, rows, LANES), wide(group, TILE, LANES),
            dma((REDUCE_SENDS,)), dma((2,)), dma((X,)), dma((Z,)), dma((Y,)), dma((group,)),
        ],
        compiler_params=pltpu.CompilerParams(collective_id=1, has_side_effects=True),
    )(loss, cont, weight)
    return losses.reshape(-1), contributions.reshape(-1), shortfall[0, 0]


def solution(mesh):
    placed = (P("obl", "scen"), P("obl", "scen"), P("obl"), P("obl"), P("obl"), P(), P("scen"))
    return jax.shard_map(
        local, mesh=mesh, in_specs=placed, out_specs=(P("scen"), P("obl"), P()), check_vma=False
    )
```

```python
import functools

import jax
import jax.numpy as jnp
import numpy as np
from jax import lax
from jax.experimental import pallas as pl
from jax.experimental.pallas import tpu as pltpu
from jax.sharding import PartitionSpec as P

LANES = 128
ROWS = 256
COLS = 512

SCALE = float(2.0**-3.4)
OFFSET = float(5.2 * 2.0**-3.4)
COEFFS = (
    -24.48703166417573,
    -58.39165125696405,
    -57.73044940308441,
    -31.529938430810628,
    -11.50559434722367,
    -3.36061823149743,
    -0.771910203459282,
    -0.15406865262823627,
    -0.033933149049334255,
)


MESH = pl.DeviceIdType.MESH
X, Z, Y, CORES = 4, 4, 4, 2
TILE = 8


def place():
    obl, scen = lax.axis_index("obl"), lax.axis_index("scen")
    return obl // X, obl % X, scen // (Z * CORES), scen // CORES % Z, scen % CORES


def obl_at(far, x):
    return far * X + x


def scen_at(y, z, core):
    return (y * Z + z) * CORES + core


class Links:
    def __init__(self, send_sems):
        self.sems, self.started = send_sems, []

    def send(self, source, target, recv_sem, obl, scen):
        copy = pltpu.make_async_remote_copy(
            src_ref=source, dst_ref=target, send_sem=self.sems.at[len(self.started)],
            recv_sem=recv_sem, device_id={"obl": obl, "scen": scen}, device_id_type=MESH,
        )
        copy.start()
        self.started.append(copy)

    def receive(self, target, recv_sem):
        pltpu.make_async_remote_copy(
            src_ref=target, dst_ref=target, send_sem=self.sems.at[0], recv_sem=recv_sem,
            device_id={"obl": lax.axis_index("obl"), "scen": lax.axis_index("scen")},
            device_id_type=MESH,
        ).wait_recv()

    def finish(self):
        for copy in self.started:
            copy.wait_send()


PIECES = 4
GATHER_SENDS = 3 + 4 + 4 + 8 + 3 + 9 + 16 + 8 + 8 + 4
REDUCE_SENDS = 2 + 3 + 3 + 3 + 31


def meet(peers):
    barrier = pltpu.get_barrier_semaphore()
    for obl, scen in peers:
        pl.semaphore_signal(
            barrier, inc=1, device_id={"obl": obl, "scen": scen}, device_id_type=MESH)
    pl.semaphore_wait(barrier, len(peers))


def gather(
    loads, scenarios, lt3, panel, passing, send_sems, local_sem, panel_sem, loads_sem, passing_sem,
):
    far, x, y, z, core = place()
    obl, scen = lax.axis_index("obl"), lax.axis_index("scen")
    height, nsc = scenarios.shape
    nobl = loads.shape[1]
    width, half_w = nsc // PIECES, nobl // 2
    right, left = (x + 1) % X, (x + X - 1) % X
    up, down = (y + 1) % Y, (y + Y - 1) % Y

    def along(step):
        other = (far * Z + z + step) % (2 * Z)
        return obl_at(other // Z, x), scen_at(y, other % Z, core)

    ways = [along(2), along(2 * Z - 2)]
    meet(
        [(obl_at(1 - far, x), scen), (obl_at(far, left), scen), (obl_at(far, right), scen)]
        + [(obl, scen_at(to, z, core)) for to in (up, down)]
        + [(obl, scen_at(y, (z + k) % Z, core)) for k in range(1, Z)]
        + [(obl, scen_at(y, z, 1 - core))]
        + ways
    )
    links = Links(send_sems)

    def columns(c):
        return slice(c * width, (c + 1) * width)

    def piece(owner, c):
        return panel.at[pl.ds(pl.multiple_of(owner * height, height), height), columns(c)]

    own_rows = pltpu.make_async_copy(
        scenarios, panel.at[pl.ds(pl.multiple_of(obl * height, height), height), :], local_sem.at[0])
    own_loads = pltpu.make_async_copy(loads, lt3.at[scen], local_sem.at[1])
    own_rows.start()
    own_loads.start()

    def panel_out(source, owner, c):
        for to in (right, left):
            links.send(source, piece(owner, c), panel_sem.at[owner, c], obl_at(far, to), scen)

    def panel_relay(row, c):
        owner = obl_at(row, right if c % 2 else left)
        links.receive(piece(owner, c), panel_sem.at[owner, c])
        links.send(
            piece(owner, c), piece(owner, c), panel_sem.at[owner, c],
            obl_at(far, left if c % 2 else right), scen)

    def panel_last(row):
        for c in range(PIECES):
            owner = obl_at(row, left if c % 2 else right)
            links.receive(piece(owner, c), panel_sem.at[owner, c])
        across = obl_at(row, (x + 2) % X)
        for c in range(PIECES):
            links.receive(piece(across, c), panel_sem.at[across, c])

    def strip(owner, part=None):
        if part is None:
            return lt3.at[owner]
        return lt3.at[owner, :, pl.ds(part * half_w, half_w)]

    def loads_out(source, owner):
        for to in (up, down):
            links.send(source, strip(owner), loads_sem.at[owner, 0], obl, scen_at(to, z, core))
        loads_across(source, owner)

    def loads_across(source, owner):
        links.send(source, strip(owner), loads_sem.at[owner, 0], obl, scen_at(y, z, 1 - core))

    def loads_relay(run):
        low, high = scen_at(down, run, core), scen_at(up, run, core)
        links.receive(strip(low), loads_sem.at[low, 0])
        links.send(strip(low, 0), strip(low, 0), loads_sem.at[low, 0], obl, scen_at(up, z, core))
        loads_across(strip(low), low)
        links.receive(strip(high), loads_sem.at[high, 0])
        links.send(strip(high, 1), strip(high, 1), loads_sem.at[high, 1], obl, scen_at(down, z, core))
        loads_across(strip(high), high)

    def loads_last(run):
        opposite = scen_at((y + 2) % Y, run, core)
        links.receive(strip(opposite, 0), loads_sem.at[opposite, 0])
        links.receive(strip(opposite, 1), loads_sem.at[opposite, 1])
        loads_across(strip(opposite), opposite)

    runs = [(z + k) % Z for k in range(Z)]
    for run in runs[1:]:
        links.send(loads, strip(scen), loads_sem.at[scen, 0], obl, scen_at(y, run, core))
    for c in range(PIECES):
        links.send(scenarios.at[:, columns(c)], passing.at[c], passing_sem.at[c], *ways[c % 2])
    for c in range(PIECES):
        panel_out(scenarios.at[:, columns(c)], obl, c)
    loads_out(loads, scen)
    for run in runs[1:]:
        owner = scen_at(y, run, core)
        links.receive(strip(owner), loads_sem.at[owner, 0])
        loads_out(strip(owner), owner)
    other = obl_at(1 - far, x)
    for c in range(PIECES):
        links.receive(passing.at[c], passing_sem.at[c])
        origin = ways[1 - c % 2][0]
        links.send(passing.at[c], piece(origin, c), panel_sem.at[origin, c], *ways[c % 2])
    loads_relay(runs[0])
    for c in range(PIECES):
        panel_relay(far, c)
    for c in range(PIECES):
        links.receive(piece(other, c), panel_sem.at[other, c])
        panel_out(piece(other, c), other, c)
        if c > 0:
            loads_relay(runs[c])
    for run in runs:
        loads_last(run)
    for c in range(PIECES):
        panel_relay(1 - far, c)
    for run in range(Z):
        for k in range(Y):
            owner = scen_at(k, run, 1 - core)
            links.receive(strip(owner), loads_sem.at[owner, 0])
    own_rows.wait()
    own_loads.wait()
    panel_last(far)
    panel_last(1 - far)
    links.finish()


def reduce(
    loss_a, cont_a, weight, losses_out, cont_out, scalars_out,
    loss_z, loss_x, cont_c, cont_z, cont_y, tiles,
    send_sems, sums_sem, loss_sem, run_sem, y_sem, tile_sem,
):
    far, x, y, z, core = place()
    obl, scen = lax.axis_index("obl"), lax.axis_index("scen")
    nrows = losses_out.shape[0]
    group = Y * Z * CORES
    meet(
        [(obl_at(1 - far, x), scen)]
        + [(obl_at(far, (x + k) % X), scen) for k in range(1, X)]
        + [(obl, (scen + k) % group) for k in range(1, group)]
    )
    links = Links(send_sems)
    weights = weight[...].astype(jnp.float32)
    weight_sum = jnp.sum(jnp.sum(weights, axis=0, keepdims=True), axis=1, keepdims=True)

    links.send(loss_a, loss_z, sums_sem.at[0], obl_at(1 - far, x), scen)
    links.send(cont_a, cont_c, sums_sem.at[1], obl, scen_at(y, z, 1 - core))
    links.receive(cont_c, sums_sem.at[1])
    cont_z[z] = cont_a[...] + cont_c[...]
    for k in range(1, Z):
        links.send(cont_z.at[z], cont_z.at[z], run_sem.at[z], obl, scen_at(y, (z + k) % Z, core))
    links.receive(loss_z, sums_sem.at[0])
    loss_x[x] = loss_a[...] + loss_z[...]
    for k in range(1, X):
        links.send(loss_x.at[x], loss_x.at[x], loss_sem.at[x], obl_at(far, (x + k) % X), scen)
    for k in range(1, Z):
        links.receive(cont_z.at[(z + k) % Z], run_sem.at[(z + k) % Z])
    cont_y[y] = cont_z[0] + cont_z[1] + cont_z[2] + cont_z[3]
    for k in range(1, Y):
        links.send(cont_y.at[y], cont_y.at[y], y_sem.at[y], obl, scen_at((y + k) % Y, z, core))
    for k in range(1, X):
        links.receive(loss_x.at[(x + k) % X], loss_sem.at[(x + k) % X])
    whole = loss_x[0] + loss_x[1] + loss_x[2] + loss_x[3]
    losses_out[...] = whole[:nrows]
    upper = lax.broadcasted_iota(jnp.int32, (TILE, LANES), 0) < TILE // 2
    tiles[scen] = jnp.where(upper, whole[nrows:], jnp.broadcast_to(weight_sum, (TILE, LANES)))
    for k in range(1, group):
        links.send(tiles.at[scen], tiles.at[scen], tile_sem.at[scen], obl, (scen + k) % group)
    for k in range(1, Y):
        links.receive(cont_y.at[(y + k) % Y], y_sem.at[(y + k) % Y])
    numer = cont_y[0] + cont_y[1] + cont_y[2] + cont_y[3]
    for k in range(1, group):
        links.receive(tiles.at[(scen + k) % group], tile_sem.at[(scen + k) % group])
    cont_out[...] = numer
    scalars_out[...] = jnp.sum(tiles[...], axis=0)
    links.finish()


def finish(count, loss, numer, scalars, losses_out, cont_out, short_out):
    total = scalars[TILE - 1 : TILE, :]
    losses_out[...] = loss[...] / count
    cont_out[...] = numer[...] / total
    short_out[0, 0] = (scalars[0:1, :] / total / count)[0, 0]


def scenario_losses(
    thresholds, lt3, panel, rho, exposure, rating, weight, loss_out, cont_out,
    lt, st, wide_weight, loss, cont, shift, slope, expo, base, prod_a, prod_b,
):
    factors, nobl = lt.shape
    nsc = panel.shape[1]

    for r in range(nobl // LANES):
        at = slice(r * LANES, (r + 1) * LANES)
        square = jnp.zeros((TILE, LANES), jnp.float32)
        for k in range(0, factors // TILE, 2):
            one, two = lt3[k, :, at].astype(jnp.float32), lt3[k + 1, :, at].astype(jnp.float32)
            square = square + one * one + two * two
            lt[k * TILE : (k + 2) * TILE, at] = jnp.concatenate([one, two], axis=0).astype(jnp.bfloat16)
        slope[r : r + 1, :] = jnp.sum(square, axis=0, keepdims=True)
    kind = rating[...]
    thr = jnp.zeros(kind.shape, jnp.float32)
    for k in range(thresholds.shape[0]):
        thr = jnp.where(kind == k, thresholds[k], thr)
    root_rest = jnp.sqrt(1.0 - rho[...])
    scale = lax.rsqrt(slope[...] + 1e-06)
    shift[...] = thr / root_rest * SCALE
    slope[...] = -(jnp.sqrt(rho[...]) * scale / root_rest) * SCALE
    expo[...] = exposure[...]
    base[...] = jnp.log2(exposure[...]) + COEFFS[0]

    @pl.loop(0, nsc // LANES)
    def _(r):
        at = pl.ds(pl.multiple_of(r * LANES, LANES), LANES)
        st[at, :] = panel[:, at].T
        row = weight[pl.ds(r, 1), :].astype(jnp.float32)
        wide_weight[at, :] = jnp.broadcast_to(row, (LANES, LANES)).T

    loss[...] = jnp.zeros_like(loss)
    cont[...] = jnp.zeros_like(cont)
    per = nsc // ROWS
    steps = per * (nobl // COLS)

    def product(step, into):
        jb, ib = step // per, step % per
        rows = pl.ds(pl.multiple_of(ib * ROWS, ROWS), ROWS)
        cols = pl.ds(pl.multiple_of(jb * COLS, COLS), COLS)
        into[...] = jnp.dot(st[rows, :], lt[:, cols], preferred_element_type=jnp.float32)

    tiles = COLS // LANES

    def spread(ref, jb):
        return [jnp.broadcast_to(ref[pl.ds(jb * tiles + j, 1), :], (8, LANES)) for j in range(tiles)]

    def reduce_step(step, prod):
        jb, ib = step // per, step % per
        a, b, e, g = spread(shift, jb), spread(slope, jb), spread(expo, jb), spread(base, jb)
        total = [jnp.zeros((8, LANES), jnp.float32) for _ in range(tiles)]
        for r in range(ROWS // 8):
            at = pl.ds(pl.multiple_of(ib * ROWS + r * 8, 8), 8)
            w = wide_weight[at, :]
            partial = None
            for j in range(tiles):
                v = prod[r * 8 : r * 8 + 8, j * LANES : (j + 1) * LANES] * b[j] + a[j]
                y = jnp.log2(jnp.abs(v) + OFFSET)
                q = y * COEFFS[-1] + COEFFS[-2]
                for c in COEFFS[-3:0:-1]:
                    q = q * y + c
                tail = jnp.exp2(q * y + g[j])
                x = jnp.where(v < 0.0, tail, e[j] - tail)
                total[j] = total[j] + x * w
                partial = x if partial is None else partial + x
            loss[at, :] = loss[at, :] + partial
        for j in range(tiles):
            at = pl.ds(pl.multiple_of(jb * COLS + j * LANES, LANES), LANES)
            cont[:, at] = cont[:, at] + total[j]

    product(0, prod_a)

    @pl.loop(0, steps // 2)
    def _(k):
        product(2 * k + 1, prod_b)
        reduce_step(2 * k, prod_a)
        product(jnp.minimum(2 * k + 2, steps - 1), prod_a)
        reduce_step(2 * k + 1, prod_b)

    for r in range(nsc // LANES):
        loss_out[r : r + 1, :] = jnp.sum(loss[r * LANES : (r + 1) * LANES, :].T, axis=0, keepdims=True)
    for r in range(nobl // LANES):
        cont_out[r : r + 1, :] = jnp.sum(cont[:, r * LANES : (r + 1) * LANES], axis=0, keepdims=True)
    numer_here = jnp.sum(jnp.sum(cont_out[...], axis=0, keepdims=True), axis=1, keepdims=True)
    loss_out[nsc // LANES :, :] = jnp.broadcast_to(numer_here, (TILE, LANES))


def local(loadings, scenarios, rho, exposure, rating, thresholds, tail_weight):
    nobl, nsc = loadings.shape[0], scenarios.shape[1]
    far_x, group = lax.axis_size("obl"), lax.axis_size("scen")
    factors = scenarios.shape[0] * far_x
    count = nobl * far_x
    rows, cols = nobl // LANES, nsc // LANES
    vmem = pl.BlockSpec(memory_space=pltpu.VMEM)
    f32, bf16, dma = jnp.float32, jnp.bfloat16, pltpu.SemaphoreType.DMA
    weight = tail_weight.reshape(cols, LANES)

    def wide(*shape):
        return pltpu.VMEM(shape, f32)

    lt3, panel = pl.pallas_call(
        gather,
        name="gather",
        out_shape=(
            jax.ShapeDtypeStruct((group, factors // group, nobl), bf16),
            jax.ShapeDtypeStruct((factors, nsc), bf16),
        ),
        in_specs=[vmem] * 2,
        out_specs=(vmem, vmem),
        scratch_shapes=[
            pltpu.VMEM((PIECES, scenarios.shape[0], nsc // PIECES), bf16),
            dma((GATHER_SENDS,)), dma((2,)), dma((far_x, PIECES)), dma((group, 2)), dma((PIECES,)),
        ],
        compiler_params=pltpu.CompilerParams(collective_id=0, has_side_effects=True),
    )(loadings.T, scenarios)
    loss, cont = pl.pallas_call(
        scenario_losses,
        name="scenario_losses",
        out_shape=(
            jax.ShapeDtypeStruct((cols + TILE, LANES), f32),
            jax.ShapeDtypeStruct((rows, LANES), f32),
        ),
        in_specs=[pl.BlockSpec(memory_space=pltpu.SMEM)] + [vmem] * 6,
        out_specs=(vmem, vmem),
        scratch_shapes=[
            pltpu.VMEM((factors, nobl), bf16),
            pltpu.VMEM((nsc, factors), bf16),
            wide(nsc, LANES), wide(nsc, LANES), wide(8, nobl),
            wide(rows, LANES), wide(rows, LANES), wide(rows, LANES), wide(rows, LANES),
            wide(ROWS, COLS), wide(ROWS, COLS),
        ],
    )(
        thresholds, lt3, panel, rho.reshape(rows, LANES), exposure.reshape(rows, LANES),
        rating.reshape(rows, LANES), weight,
    )
    losses, contributions, shortfall = pl.pallas_call(
        reduce,
        name="reduce",
        out_shape=(
            jax.ShapeDtypeStruct((cols, LANES), f32),
            jax.ShapeDtypeStruct((rows, LANES), f32),
            jax.ShapeDtypeStruct((TILE, LANES), f32),
        ),
        in_specs=[vmem] * 3,
        out_specs=(vmem, vmem, vmem),
        scratch_shapes=[
            wide(cols + TILE, LANES), wide(X, cols + TILE, LANES),
            wide(rows, LANES), wide(Z, rows, LANES), wide(Y, rows, LANES), wide(group, TILE, LANES),
            dma((REDUCE_SENDS,)), dma((2,)), dma((X,)), dma((Z,)), dma((Y,)), dma((group,)),
        ],
        compiler_params=pltpu.CompilerParams(collective_id=1, has_side_effects=True),
    )(loss, cont, weight)
    losses, contributions, shortfall = pl.pallas_call(
        functools.partial(finish, count),
        name="finish",
        out_shape=(
            jax.ShapeDtypeStruct((cols, LANES), f32),
            jax.ShapeDtypeStruct((rows, LANES), f32),
            jax.ShapeDtypeStruct((1, 1), f32),
        ),
        in_specs=[vmem] * 3,
        out_specs=(vmem, vmem, pl.BlockSpec(memory_space=pltpu.SMEM)),
    )(losses, contributions, shortfall)
    return losses.reshape(-1), contributions.reshape(-1), shortfall.reshape(())


def solution(mesh):
    placed = (P("obl", "scen"), P("obl", "scen"), P("obl"), P("obl"), P("obl"), P(), P("scen"))
    return jax.shard_map(
        local, mesh=mesh, in_specs=placed, out_specs=(P("scen"), P("obl"), P()), check_vma=False
    )
```

```python
import functools

import jax
import jax.numpy as jnp
import numpy as np
from jax import lax
from jax.experimental import pallas as pl
from jax.experimental.pallas import tpu as pltpu
from jax.sharding import PartitionSpec as P

LANES = 128
ROWS = 512
COLS = 512

SCALE = float(2.0**-3.4)
OFFSET = float(5.2 * 2.0**-3.4)
COEFFS = (
    -24.48703166417573,
    -58.39165125696405,
    -57.73044940308441,
    -31.529938430810628,
    -11.50559434722367,
    -3.36061823149743,
    -0.771910203459282,
    -0.15406865262823627,
    -0.033933149049334255,
)


MESH = pl.DeviceIdType.MESH
X, Z, Y, CORES = 4, 4, 4, 2
TILE = 8


def place():
    obl, scen = lax.axis_index("obl"), lax.axis_index("scen")
    return obl // X, obl % X, scen // (Z * CORES), scen // CORES % Z, scen % CORES


def obl_at(far, x):
    return far * X + x


def scen_at(y, z, core):
    return (y * Z + z) * CORES + core


class Links:
    def __init__(self, send_sems):
        self.sems, self.started = send_sems, []

    def send(self, source, target, recv_sem, obl, scen):
        copy = pltpu.make_async_remote_copy(
            src_ref=source, dst_ref=target, send_sem=self.sems.at[len(self.started)],
            recv_sem=recv_sem, device_id={"obl": obl, "scen": scen}, device_id_type=MESH,
        )
        copy.start()
        self.started.append(copy)

    def receive(self, target, recv_sem):
        pltpu.make_async_remote_copy(
            src_ref=target, dst_ref=target, send_sem=self.sems.at[0], recv_sem=recv_sem,
            device_id={"obl": lax.axis_index("obl"), "scen": lax.axis_index("scen")},
            device_id_type=MESH,
        ).wait_recv()

    def finish(self):
        for copy in self.started:
            copy.wait_send()


PIECES = 4
GATHER_SENDS = 3 + 4 + 4 + 8 + 3 + 9 + 16 + 8 + 8 + 4
REDUCE_SENDS = 2 + 3 + 3 + 3 + 31


def meet(peers):
    barrier = pltpu.get_barrier_semaphore()
    for obl, scen in peers:
        pl.semaphore_signal(
            barrier, inc=1, device_id={"obl": obl, "scen": scen}, device_id_type=MESH)
    pl.semaphore_wait(barrier, len(peers))


def gather(
    loads, scenarios, lt3, panel, passing, send_sems, local_sem, panel_sem, loads_sem, passing_sem,
):
    far, x, y, z, core = place()
    obl, scen = lax.axis_index("obl"), lax.axis_index("scen")
    height, nsc = scenarios.shape
    nobl = loads.shape[1]
    width, half_w = nsc // PIECES, nobl // 2
    right, left = (x + 1) % X, (x + X - 1) % X
    up, down = (y + 1) % Y, (y + Y - 1) % Y

    def along(step):
        other = (far * Z + z + step) % (2 * Z)
        return obl_at(other // Z, x), scen_at(y, other % Z, core)

    ways = [along(2), along(2 * Z - 2)]
    meet(
        [(obl_at(far, left), scen), (obl_at(far, right), scen)]
        + [(obl, scen_at(to, z, core)) for to in (up, down)]
        + [(obl, scen_at(y, (z + k) % Z, core)) for k in range(1, Z)]
        + [(obl, scen_at(y, z, 1 - core))]
        + ways
    )
    links = Links(send_sems)

    def columns(c):
        return slice(c * width, (c + 1) * width)

    def piece(owner, c):
        return panel.at[pl.ds(pl.multiple_of(owner * height, height), height), columns(c)]

    own_rows = pltpu.make_async_copy(
        scenarios, panel.at[pl.ds(pl.multiple_of(obl * height, height), height), :], local_sem.at[0])
    own_loads = pltpu.make_async_copy(loads, lt3.at[scen], local_sem.at[1])
    own_rows.start()
    own_loads.start()

    def panel_out(source, owner, c):
        for to in (right, left):
            links.send(source, piece(owner, c), panel_sem.at[owner, c], obl_at(far, to), scen)

    def panel_relay(row, c):
        owner = obl_at(row, right if c % 2 else left)
        links.receive(piece(owner, c), panel_sem.at[owner, c])
        links.send(
            piece(owner, c), piece(owner, c), panel_sem.at[owner, c],
            obl_at(far, left if c % 2 else right), scen)

    def panel_last(row):
        for c in range(PIECES):
            owner = obl_at(row, left if c % 2 else right)
            links.receive(piece(owner, c), panel_sem.at[owner, c])
        across = obl_at(row, (x + 2) % X)
        for c in range(PIECES):
            links.receive(piece(across, c), panel_sem.at[across, c])

    def strip(owner, part=None):
        if part is None:
            return lt3.at[owner]
        return lt3.at[owner, :, pl.ds(part * half_w, half_w)]

    def loads_out(source, owner):
        for to in (up, down):
            links.send(source, strip(owner), loads_sem.at[owner, 0], obl, scen_at(to, z, core))
        loads_across(source, owner)

    def loads_across(source, owner):
        links.send(source, strip(owner), loads_sem.at[owner, 0], obl, scen_at(y, z, 1 - core))

    def loads_relay(run):
        low, high = scen_at(down, run, core), scen_at(up, run, core)
        links.receive(strip(low), loads_sem.at[low, 0])
        links.send(strip(low, 0), strip(low, 0), loads_sem.at[low, 0], obl, scen_at(up, z, core))
        loads_across(strip(low), low)
        links.receive(strip(high), loads_sem.at[high, 0])
        links.send(strip(high, 1), strip(high, 1), loads_sem.at[high, 1], obl, scen_at(down, z, core))
        loads_across(strip(high), high)

    def loads_last(run):
        opposite = scen_at((y + 2) % Y, run, core)
        links.receive(strip(opposite, 0), loads_sem.at[opposite, 0])
        links.receive(strip(opposite, 1), loads_sem.at[opposite, 1])
        loads_across(strip(opposite), opposite)

    runs = [(z + k) % Z for k in range(Z)]
    for run in runs[1:]:
        links.send(loads, strip(scen), loads_sem.at[scen, 0], obl, scen_at(y, run, core))
    for c in range(PIECES):
        links.send(scenarios.at[:, columns(c)], passing.at[c], passing_sem.at[c], *ways[c % 2])
    for c in range(PIECES):
        panel_out(scenarios.at[:, columns(c)], obl, c)
    loads_out(loads, scen)
    for run in runs[1:]:
        owner = scen_at(y, run, core)
        links.receive(strip(owner), loads_sem.at[owner, 0])
        loads_out(strip(owner), owner)
    other = obl_at(1 - far, x)
    for c in range(PIECES):
        links.receive(passing.at[c], passing_sem.at[c])
        origin = ways[1 - c % 2][0]
        links.send(passing.at[c], piece(origin, c), panel_sem.at[origin, c], *ways[c % 2])
    loads_relay(runs[0])
    for c in range(PIECES):
        panel_relay(far, c)
    for c in range(PIECES):
        links.receive(piece(other, c), panel_sem.at[other, c])
        panel_out(piece(other, c), other, c)
        if c > 0:
            panel_relay(1 - far, c - 1)
            loads_relay(runs[c])
    panel_relay(1 - far, PIECES - 1)
    for run in runs:
        loads_last(run)
    for run in range(Z):
        for k in range(Y):
            owner = scen_at(k, run, 1 - core)
            links.receive(strip(owner), loads_sem.at[owner, 0])
    own_rows.wait()
    own_loads.wait()
    panel_last(far)
    panel_last(1 - far)
    links.finish()


def reduce(
    loss_a, cont_a, weight, losses_out, cont_out, scalars_out,
    loss_z, loss_x, cont_c, cont_z, cont_y, tiles,
    send_sems, sums_sem, loss_sem, run_sem, y_sem, tile_sem,
):
    far, x, y, z, core = place()
    obl, scen = lax.axis_index("obl"), lax.axis_index("scen")
    nrows = losses_out.shape[0]
    group = Y * Z * CORES
    meet(
        [(obl_at(1 - far, x), scen)]
        + [(obl_at(far, (x + k) % X), scen) for k in range(1, X)]
        + [(obl, (scen + k) % group) for k in range(1, group)]
    )
    links = Links(send_sems)
    weights = weight[...].astype(jnp.float32)
    weight_sum = jnp.sum(jnp.sum(weights, axis=0, keepdims=True), axis=1, keepdims=True)

    links.send(loss_a, loss_z, sums_sem.at[0], obl_at(1 - far, x), scen)
    links.send(cont_a, cont_c, sums_sem.at[1], obl, scen_at(y, z, 1 - core))
    links.receive(cont_c, sums_sem.at[1])
    cont_z[z] = cont_a[...] + cont_c[...]
    for k in range(1, Z):
        links.send(cont_z.at[z], cont_z.at[z], run_sem.at[z], obl, scen_at(y, (z + k) % Z, core))
    links.receive(loss_z, sums_sem.at[0])
    loss_x[x] = loss_a[...] + loss_z[...]
    for k in range(1, X):
        links.send(loss_x.at[x], loss_x.at[x], loss_sem.at[x], obl_at(far, (x + k) % X), scen)
    for k in range(1, Z):
        links.receive(cont_z.at[(z + k) % Z], run_sem.at[(z + k) % Z])
    cont_y[y] = cont_z[0] + cont_z[1] + cont_z[2] + cont_z[3]
    for k in range(1, Y):
        links.send(cont_y.at[y], cont_y.at[y], y_sem.at[y], obl, scen_at((y + k) % Y, z, core))
    for k in range(1, X):
        links.receive(loss_x.at[(x + k) % X], loss_sem.at[(x + k) % X])
    whole = loss_x[0] + loss_x[1] + loss_x[2] + loss_x[3]
    losses_out[...] = whole[:nrows]
    upper = lax.broadcasted_iota(jnp.int32, (TILE, LANES), 0) < TILE // 2
    tiles[scen] = jnp.where(upper, whole[nrows:], jnp.broadcast_to(weight_sum, (TILE, LANES)))
    for k in range(1, group):
        links.send(tiles.at[scen], tiles.at[scen], tile_sem.at[scen], obl, (scen + k) % group)
    for k in range(1, Y):
        links.receive(cont_y.at[(y + k) % Y], y_sem.at[(y + k) % Y])
    numer = cont_y[0] + cont_y[1] + cont_y[2] + cont_y[3]
    for k in range(1, group):
        links.receive(tiles.at[(scen + k) % group], tile_sem.at[(scen + k) % group])
    cont_out[...] = numer
    scalars_out[...] = jnp.sum(tiles[...], axis=0)
    links.finish()


def finish(count, loss, numer, scalars, losses_out, cont_out, short_out):
    total = scalars[TILE - 1 : TILE, :]
    losses_out[...] = loss[...] / count
    cont_out[...] = numer[...] / total
    short_out[0, 0] = (scalars[0:1, :] / total / count)[0, 0]


def scenario_losses(
    thresholds, lt3, panel, rho, exposure, rating, weight, loss_out, cont_out,
    lt, st, wide_weight, loss, cont, shift, slope, expo, base, prod_a, prod_b,
):
    factors, nobl = lt.shape
    nsc = panel.shape[1]

    for r in range(nobl // LANES):
        at = slice(r * LANES, (r + 1) * LANES)
        square = jnp.zeros((TILE, LANES), jnp.float32)
        for k in range(0, factors // TILE, 2):
            one, two = lt3[k, :, at].astype(jnp.float32), lt3[k + 1, :, at].astype(jnp.float32)
            square = square + one * one + two * two
            lt[k * TILE : (k + 2) * TILE, at] = jnp.concatenate([one, two], axis=0).astype(jnp.bfloat16)
        slope[r : r + 1, :] = jnp.sum(square, axis=0, keepdims=True)
    kind = rating[...]
    thr = jnp.zeros(kind.shape, jnp.float32)
    for k in range(thresholds.shape[0]):
        thr = jnp.where(kind == k, thresholds[k], thr)
    root_rest = jnp.sqrt(1.0 - rho[...])
    scale = lax.rsqrt(slope[...] + 1e-06)
    shift[...] = thr / root_rest * SCALE
    slope[...] = -(jnp.sqrt(rho[...]) * scale / root_rest) * SCALE
    expo[...] = exposure[...]
    base[...] = jnp.log2(exposure[...]) + COEFFS[0]

    @pl.loop(0, nsc // LANES)
    def _(r):
        at = pl.ds(pl.multiple_of(r * LANES, LANES), LANES)
        st[at, :] = panel[:, at].T
        row = weight[pl.ds(r, 1), :].astype(jnp.float32)
        wide_weight[at, :] = jnp.broadcast_to(row, (LANES, LANES)).T

    loss[...] = jnp.zeros_like(loss)
    cont[...] = jnp.zeros_like(cont)
    per = nsc // ROWS
    steps = per * (nobl // COLS)

    def product(step, into):
        jb, ib = step // per, step % per
        rows = pl.ds(pl.multiple_of(ib * ROWS, ROWS), ROWS)
        cols = pl.ds(pl.multiple_of(jb * COLS, COLS), COLS)
        into[...] = jnp.dot(st[rows, :], lt[:, cols], preferred_element_type=jnp.float32)

    tiles = COLS // LANES

    def spread(ref, jb):
        return [jnp.broadcast_to(ref[pl.ds(jb * tiles + j, 1), :], (8, LANES)) for j in range(tiles)]

    def reduce_step(step, prod):
        jb, ib = step // per, step % per
        a, b, e, g = spread(shift, jb), spread(slope, jb), spread(expo, jb), spread(base, jb)
        total = [jnp.zeros((8, LANES), jnp.float32) for _ in range(tiles)]
        for r in range(ROWS // 8):
            at = pl.ds(pl.multiple_of(ib * ROWS + r * 8, 8), 8)
            w = wide_weight[at, :]
            partial = None
            for j in range(tiles):
                v = prod[r * 8 : r * 8 + 8, j * LANES : (j + 1) * LANES] * b[j] + a[j]
                y = jnp.log2(jnp.abs(v) + OFFSET)
                q = y * COEFFS[-1] + COEFFS[-2]
                for c in COEFFS[-3:0:-1]:
                    q = q * y + c
                tail = jnp.exp2(q * y + g[j])
                x = jnp.where(v < 0.0, tail, e[j] - tail)
                total[j] = total[j] + x * w
                partial = x if partial is None else partial + x
            loss[at, :] = loss[at, :] + partial
        for j in range(tiles):
            at = pl.ds(pl.multiple_of(jb * COLS + j * LANES, LANES), LANES)
            cont[:, at] = cont[:, at] + total[j]

    product(0, prod_a)

    @pl.loop(0, steps // 2)
    def _(k):
        product(2 * k + 1, prod_b)
        reduce_step(2 * k, prod_a)
        product(jnp.minimum(2 * k + 2, steps - 1), prod_a)
        reduce_step(2 * k + 1, prod_b)

    for r in range(nsc // LANES):
        loss_out[r : r + 1, :] = jnp.sum(loss[r * LANES : (r + 1) * LANES, :].T, axis=0, keepdims=True)
    for r in range(nobl // LANES):
        cont_out[r : r + 1, :] = jnp.sum(cont[:, r * LANES : (r + 1) * LANES], axis=0, keepdims=True)
    numer_here = jnp.sum(jnp.sum(cont_out[...], axis=0, keepdims=True), axis=1, keepdims=True)
    loss_out[nsc // LANES :, :] = jnp.broadcast_to(numer_here, (TILE, LANES))


def local(loadings, scenarios, rho, exposure, rating, thresholds, tail_weight):
    nobl, nsc = loadings.shape[0], scenarios.shape[1]
    far_x, group = lax.axis_size("obl"), lax.axis_size("scen")
    factors = scenarios.shape[0] * far_x
    count = nobl * far_x
    rows, cols = nobl // LANES, nsc // LANES
    vmem = pl.BlockSpec(memory_space=pltpu.VMEM)
    f32, bf16, dma = jnp.float32, jnp.bfloat16, pltpu.SemaphoreType.DMA
    weight = tail_weight.reshape(cols, LANES)

    def wide(*shape):
        return pltpu.VMEM(shape, f32)

    lt3, panel = pl.pallas_call(
        gather,
        name="gather",
        out_shape=(
            jax.ShapeDtypeStruct((group, factors // group, nobl), bf16),
            jax.ShapeDtypeStruct((factors, nsc), bf16),
        ),
        in_specs=[vmem] * 2,
        out_specs=(vmem, vmem),
        scratch_shapes=[
            pltpu.VMEM((PIECES, scenarios.shape[0], nsc // PIECES), bf16),
            dma((GATHER_SENDS,)), dma((2,)), dma((far_x, PIECES)), dma((group, 2)), dma((PIECES,)),
        ],
        compiler_params=pltpu.CompilerParams(collective_id=0, has_side_effects=True),
    )(loadings.T, scenarios)
    loss, cont = pl.pallas_call(
        scenario_losses,
        name="scenario_losses",
        out_shape=(
            jax.ShapeDtypeStruct((cols + TILE, LANES), f32),
            jax.ShapeDtypeStruct((rows, LANES), f32),
        ),
        in_specs=[pl.BlockSpec(memory_space=pltpu.SMEM)] + [vmem] * 6,
        out_specs=(vmem, vmem),
        scratch_shapes=[
            pltpu.VMEM((factors, nobl), bf16),
            pltpu.VMEM((nsc, factors), bf16),
            wide(nsc, LANES), wide(nsc, LANES), wide(8, nobl),
            wide(rows, LANES), wide(rows, LANES), wide(rows, LANES), wide(rows, LANES),
            wide(ROWS, COLS), wide(ROWS, COLS),
        ],
    )(
        thresholds, lt3, panel, rho.reshape(rows, LANES), exposure.reshape(rows, LANES),
        rating.reshape(rows, LANES), weight,
    )
    losses, contributions, shortfall = pl.pallas_call(
        reduce,
        name="reduce",
        out_shape=(
            jax.ShapeDtypeStruct((cols, LANES), f32),
            jax.ShapeDtypeStruct((rows, LANES), f32),
            jax.ShapeDtypeStruct((TILE, LANES), f32),
        ),
        in_specs=[vmem] * 3,
        out_specs=(vmem, vmem, vmem),
        scratch_shapes=[
            wide(cols + TILE, LANES), wide(X, cols + TILE, LANES),
            wide(rows, LANES), wide(Z, rows, LANES), wide(Y, rows, LANES), wide(group, TILE, LANES),
            dma((REDUCE_SENDS,)), dma((2,)), dma((X,)), dma((Z,)), dma((Y,)), dma((group,)),
        ],
        compiler_params=pltpu.CompilerParams(collective_id=1, has_side_effects=True),
    )(loss, cont, weight)
    losses, contributions, shortfall = pl.pallas_call(
        functools.partial(finish, count),
        name="finish",
        out_shape=(
            jax.ShapeDtypeStruct((cols, LANES), f32),
            jax.ShapeDtypeStruct((rows, LANES), f32),
            jax.ShapeDtypeStruct((1, 1), f32),
        ),
        in_specs=[vmem] * 3,
        out_specs=(vmem, vmem, pl.BlockSpec(memory_space=pltpu.SMEM)),
    )(losses, contributions, shortfall)
    return losses.reshape(-1), contributions.reshape(-1), shortfall.reshape(())


def solution(mesh):
    placed = (P("obl", "scen"), P("obl", "scen"), P("obl"), P("obl"), P("obl"), P(), P("scen"))
    return jax.shard_map(
        local, mesh=mesh, in_specs=placed, out_specs=(P("scen"), P("obl"), P()), check_vma=False
    )
```

```python
import functools

import jax
import jax.numpy as jnp
import numpy as np
from jax import lax
from jax.experimental import pallas as pl
from jax.experimental.pallas import tpu as pltpu
from jax.sharding import PartitionSpec as P

LANES = 128
ROWS = 1024
COLS = 512

SCALE = float(2.0**-3.4)
OFFSET = float(5.2 * 2.0**-3.4)
COEFFS = (
    -24.48703166417573,
    -58.39165125696405,
    -57.73044940308441,
    -31.529938430810628,
    -11.50559434722367,
    -3.36061823149743,
    -0.771910203459282,
    -0.15406865262823627,
    -0.033933149049334255,
)


MESH = pl.DeviceIdType.MESH
X, Z, Y, CORES = 4, 4, 4, 2
TILE = 8


def place():
    obl, scen = lax.axis_index("obl"), lax.axis_index("scen")
    return obl // X, obl % X, scen // (Z * CORES), scen // CORES % Z, scen % CORES


def obl_at(far, x):
    return far * X + x


def scen_at(y, z, core):
    return (y * Z + z) * CORES + core


class Links:
    def __init__(self, send_sems):
        self.sems, self.started = send_sems, []

    def send(self, source, target, recv_sem, obl, scen):
        copy = pltpu.make_async_remote_copy(
            src_ref=source, dst_ref=target, send_sem=self.sems.at[len(self.started)],
            recv_sem=recv_sem, device_id={"obl": obl, "scen": scen}, device_id_type=MESH,
        )
        copy.start()
        self.started.append(copy)

    def receive(self, target, recv_sem):
        pltpu.make_async_remote_copy(
            src_ref=target, dst_ref=target, send_sem=self.sems.at[0], recv_sem=recv_sem,
            device_id={"obl": lax.axis_index("obl"), "scen": lax.axis_index("scen")},
            device_id_type=MESH,
        ).wait_recv()

    def finish(self):
        for copy in self.started:
            copy.wait_send()


PIECES = 4
GATHER_SENDS = 3 + 4 + 4 + 8 + 3 + 9 + 16 + 8 + 8 + 4
REDUCE_SENDS = 2 + 3 + 3 + 3 + 31


def meet(peers):
    barrier = pltpu.get_barrier_semaphore()
    for obl, scen in peers:
        pl.semaphore_signal(
            barrier, inc=1, device_id={"obl": obl, "scen": scen}, device_id_type=MESH)
    pl.semaphore_wait(barrier, len(peers))


def gather(
    loads, scenarios, lt3, panel, passing, send_sems, local_sem, panel_sem, loads_sem, passing_sem,
):
    far, x, y, z, core = place()
    obl, scen = lax.axis_index("obl"), lax.axis_index("scen")
    height, nsc = scenarios.shape
    nobl = loads.shape[1]
    width, half_w = nsc // PIECES, nobl // 2
    right, left = (x + 1) % X, (x + X - 1) % X
    up, down = (y + 1) % Y, (y + Y - 1) % Y

    def along(step):
        other = (far * Z + z + step) % (2 * Z)
        return obl_at(other // Z, x), scen_at(y, other % Z, core)

    ways = [along(2), along(2 * Z - 2)]
    meet(
        [(obl_at(far, left), scen), (obl_at(far, right), scen)]
        + [(obl, scen_at(to, z, core)) for to in (up, down)]
        + [(obl, scen_at(y, (z + k) % Z, core)) for k in range(1, Z)]
        + [(obl, scen_at(y, z, 1 - core))]
        + ways
    )
    links = Links(send_sems)

    def columns(c):
        return slice(c * width, (c + 1) * width)

    def piece(owner, c):
        return panel.at[pl.ds(pl.multiple_of(owner * height, height), height), columns(c)]

    own_rows = pltpu.make_async_copy(
        scenarios, panel.at[pl.ds(pl.multiple_of(obl * height, height), height), :], local_sem.at[0])
    own_loads = pltpu.make_async_copy(loads, lt3.at[scen], local_sem.at[1])
    own_rows.start()
    own_loads.start()

    def panel_out(source, owner, c):
        for to in (right, left):
            links.send(source, piece(owner, c), panel_sem.at[owner, c], obl_at(far, to), scen)

    def panel_relay(row, c):
        owner = obl_at(row, right if c % 2 else left)
        links.receive(piece(owner, c), panel_sem.at[owner, c])
        links.send(
            piece(owner, c), piece(owner, c), panel_sem.at[owner, c],
            obl_at(far, left if c % 2 else right), scen)

    def panel_last(row):
        for c in range(PIECES):
            owner = obl_at(row, left if c % 2 else right)
            links.receive(piece(owner, c), panel_sem.at[owner, c])
        across = obl_at(row, (x + 2) % X)
        for c in range(PIECES):
            links.receive(piece(across, c), panel_sem.at[across, c])

    def strip(owner, part=None):
        if part is None:
            return lt3.at[owner]
        return lt3.at[owner, :, pl.ds(part * half_w, half_w)]

    def loads_out(source, owner):
        for to in (up, down):
            links.send(source, strip(owner), loads_sem.at[owner, 0], obl, scen_at(to, z, core))
        loads_across(source, owner)

    def loads_across(source, owner):
        links.send(source, strip(owner), loads_sem.at[owner, 0], obl, scen_at(y, z, 1 - core))

    def loads_relay(run):
        low, high = scen_at(down, run, core), scen_at(up, run, core)
        links.receive(strip(low), loads_sem.at[low, 0])
        links.send(strip(low, 0), strip(low, 0), loads_sem.at[low, 0], obl, scen_at(up, z, core))
        loads_across(strip(low), low)
        links.receive(strip(high), loads_sem.at[high, 0])
        links.send(strip(high, 1), strip(high, 1), loads_sem.at[high, 1], obl, scen_at(down, z, core))
        loads_across(strip(high), high)

    def loads_last(run):
        opposite = scen_at((y + 2) % Y, run, core)
        links.receive(strip(opposite, 0), loads_sem.at[opposite, 0])
        links.receive(strip(opposite, 1), loads_sem.at[opposite, 1])
        loads_across(strip(opposite), opposite)

    runs = [(z + k) % Z for k in range(Z)]
    for run in runs[1:]:
        links.send(loads, strip(scen), loads_sem.at[scen, 0], obl, scen_at(y, run, core))
    for c in range(PIECES):
        links.send(scenarios.at[:, columns(c)], passing.at[c], passing_sem.at[c], *ways[c % 2])
    for c in range(PIECES):
        panel_out(scenarios.at[:, columns(c)], obl, c)
    loads_out(loads, scen)
    for run in runs[1:]:
        owner = scen_at(y, run, core)
        links.receive(strip(owner), loads_sem.at[owner, 0])
        loads_out(strip(owner), owner)
    other = obl_at(1 - far, x)
    for c in range(PIECES):
        links.receive(passing.at[c], passing_sem.at[c])
        origin = ways[1 - c % 2][0]
        links.send(passing.at[c], piece(origin, c), panel_sem.at[origin, c], *ways[c % 2])
        panel_relay(far, c)
        if c == 0:
            loads_relay(runs[0])
    for c in range(PIECES):
        links.receive(piece(other, c), panel_sem.at[other, c])
        panel_out(piece(other, c), other, c)
        if c > 0:
            panel_relay(1 - far, c - 1)
        if 0 < c < Z:
            loads_relay(runs[c])
    panel_relay(1 - far, PIECES - 1)
    for run in runs:
        loads_last(run)
    for run in range(Z):
        for k in range(Y):
            owner = scen_at(k, run, 1 - core)
            links.receive(strip(owner), loads_sem.at[owner, 0])
    own_rows.wait()
    own_loads.wait()
    panel_last(far)
    panel_last(1 - far)
    links.finish()


def reduce(
    loss_a, cont_a, weight, losses_out, cont_out, scalars_out,
    loss_z, loss_x, cont_c, cont_z, cont_y, tiles,
    send_sems, sums_sem, loss_sem, run_sem, y_sem, tile_sem,
):
    far, x, y, z, core = place()
    obl, scen = lax.axis_index("obl"), lax.axis_index("scen")
    nrows = losses_out.shape[0]
    group = Y * Z * CORES
    meet(
        [(obl_at(1 - far, x), scen)]
        + [(obl_at(far, (x + k) % X), scen) for k in range(1, X)]
        + [(obl, (scen + k) % group) for k in range(1, group)]
    )
    links = Links(send_sems)
    weights = weight[...].astype(jnp.float32)
    weight_sum = jnp.sum(jnp.sum(weights, axis=0, keepdims=True), axis=1, keepdims=True)

    links.send(loss_a, loss_z, sums_sem.at[0], obl_at(1 - far, x), scen)
    links.send(cont_a, cont_c, sums_sem.at[1], obl, scen_at(y, z, 1 - core))
    links.receive(cont_c, sums_sem.at[1])
    cont_z[z] = cont_a[...] + cont_c[...]
    for k in range(1, Z):
        links.send(cont_z.at[z], cont_z.at[z], run_sem.at[z], obl, scen_at(y, (z + k) % Z, core))
    links.receive(loss_z, sums_sem.at[0])
    loss_x[x] = loss_a[...] + loss_z[...]
    for k in range(1, X):
        links.send(loss_x.at[x], loss_x.at[x], loss_sem.at[x], obl_at(far, (x + k) % X), scen)
    for k in range(1, Z):
        links.receive(cont_z.at[(z + k) % Z], run_sem.at[(z + k) % Z])
    cont_y[y] = cont_z[0] + cont_z[1] + cont_z[2] + cont_z[3]
    for k in range(1, Y):
        links.send(cont_y.at[y], cont_y.at[y], y_sem.at[y], obl, scen_at((y + k) % Y, z, core))
    for k in range(1, X):
        links.receive(loss_x.at[(x + k) % X], loss_sem.at[(x + k) % X])
    whole = loss_x[0] + loss_x[1] + loss_x[2] + loss_x[3]
    losses_out[...] = whole[:nrows]
    upper = lax.broadcasted_iota(jnp.int32, (TILE, LANES), 0) < TILE // 2
    tiles[scen] = jnp.where(upper, whole[nrows:], jnp.broadcast_to(weight_sum, (TILE, LANES)))
    for k in range(1, group):
        links.send(tiles.at[scen], tiles.at[scen], tile_sem.at[scen], obl, (scen + k) % group)
    for k in range(1, Y):
        links.receive(cont_y.at[(y + k) % Y], y_sem.at[(y + k) % Y])
    numer = cont_y[0] + cont_y[1] + cont_y[2] + cont_y[3]
    for k in range(1, group):
        links.receive(tiles.at[(scen + k) % group], tile_sem.at[(scen + k) % group])
    cont_out[...] = numer
    scalars_out[...] = jnp.sum(tiles[...], axis=0)
    links.finish()


def finish(count, loss, numer, scalars, losses_out, cont_out, short_out):
    total = scalars[TILE - 1 : TILE, :]
    losses_out[...] = loss[...] / count
    cont_out[...] = numer[...] / total
    short_out[0, 0] = (scalars[0:1, :] / total / count)[0, 0]


def scenario_losses(
    thresholds, lt3, panel, rho, exposure, rating, weight, loss_out, cont_out,
    lt, st, wide_weight, loss, cont, shift, slope, expo, base, prod_a, prod_b,
):
    factors, nobl = lt.shape
    nsc = panel.shape[1]

    for r in range(nobl // LANES):
        at = slice(r * LANES, (r + 1) * LANES)
        square = jnp.zeros((TILE, LANES), jnp.float32)
        for k in range(0, factors // TILE, 2):
            one, two = lt3[k, :, at].astype(jnp.float32), lt3[k + 1, :, at].astype(jnp.float32)
            square = square + one * one + two * two
            lt[k * TILE : (k + 2) * TILE, at] = jnp.concatenate([one, two], axis=0).astype(jnp.bfloat16)
        slope[r : r + 1, :] = jnp.sum(square, axis=0, keepdims=True)
    kind = rating[...]
    thr = jnp.zeros(kind.shape, jnp.float32)
    for k in range(thresholds.shape[0]):
        thr = jnp.where(kind == k, thresholds[k], thr)
    root_rest = jnp.sqrt(1.0 - rho[...])
    scale = lax.rsqrt(slope[...] + 1e-06)
    shift[...] = thr / root_rest * SCALE
    slope[...] = -(jnp.sqrt(rho[...]) * scale / root_rest) * SCALE
    expo[...] = exposure[...]
    base[...] = jnp.log2(exposure[...]) + COEFFS[0]

    @pl.loop(0, nsc // LANES)
    def _(r):
        at = pl.ds(pl.multiple_of(r * LANES, LANES), LANES)
        st[at, :] = panel[:, at].T
        row = weight[pl.ds(r, 1), :].astype(jnp.float32)
        wide_weight[at, :] = jnp.broadcast_to(row, (LANES, LANES)).T

    loss[...] = jnp.zeros_like(loss)
    cont[...] = jnp.zeros_like(cont)
    per = nsc // ROWS
    steps = per * (nobl // COLS)

    def product(step, into):
        jb, ib = step // per, step % per
        rows = pl.ds(pl.multiple_of(ib * ROWS, ROWS), ROWS)
        cols = pl.ds(pl.multiple_of(jb * COLS, COLS), COLS)
        into[...] = jnp.dot(st[rows, :], lt[:, cols], preferred_element_type=jnp.float32)

    tiles = COLS // LANES

    def spread(ref, jb):
        return [jnp.broadcast_to(ref[pl.ds(jb * tiles + j, 1), :], (8, LANES)) for j in range(tiles)]

    def reduce_step(step, prod):
        jb, ib = step // per, step % per
        a, b, e, g = spread(shift, jb), spread(slope, jb), spread(expo, jb), spread(base, jb)
        total = [jnp.zeros((8, LANES), jnp.float32) for _ in range(tiles)]
        for r in range(ROWS // 8):
            at = pl.ds(pl.multiple_of(ib * ROWS + r * 8, 8), 8)
            w = wide_weight[at, :]
            partial = None
            for j in range(tiles):
                v = prod[r * 8 : r * 8 + 8, j * LANES : (j + 1) * LANES] * b[j] + a[j]
                y = jnp.log2(jnp.abs(v) + OFFSET)
                q = y * COEFFS[-1] + COEFFS[-2]
                for c in COEFFS[-3:0:-1]:
                    q = q * y + c
                tail = jnp.exp2(q * y + g[j])
                x = jnp.where(v < 0.0, tail, e[j] - tail)
                total[j] = total[j] + x * w
                partial = x if partial is None else partial + x
            loss[at, :] = loss[at, :] + partial
        for j in range(tiles):
            at = pl.ds(pl.multiple_of(jb * COLS + j * LANES, LANES), LANES)
            cont[:, at] = cont[:, at] + total[j]

    product(0, prod_a)

    @pl.loop(0, steps // 2)
    def _(k):
        product(2 * k + 1, prod_b)
        reduce_step(2 * k, prod_a)
        product(jnp.minimum(2 * k + 2, steps - 1), prod_a)
        reduce_step(2 * k + 1, prod_b)

    for r in range(nsc // LANES):
        loss_out[r : r + 1, :] = jnp.sum(loss[r * LANES : (r + 1) * LANES, :].T, axis=0, keepdims=True)
    for r in range(nobl // LANES):
        cont_out[r : r + 1, :] = jnp.sum(cont[:, r * LANES : (r + 1) * LANES], axis=0, keepdims=True)
    numer_here = jnp.sum(jnp.sum(cont_out[...], axis=0, keepdims=True), axis=1, keepdims=True)
    loss_out[nsc // LANES :, :] = jnp.broadcast_to(numer_here, (TILE, LANES))


def local(loadings, scenarios, rho, exposure, rating, thresholds, tail_weight):
    nobl, nsc = loadings.shape[0], scenarios.shape[1]
    far_x, group = lax.axis_size("obl"), lax.axis_size("scen")
    factors = scenarios.shape[0] * far_x
    count = nobl * far_x
    rows, cols = nobl // LANES, nsc // LANES
    vmem = pl.BlockSpec(memory_space=pltpu.VMEM)
    f32, bf16, dma = jnp.float32, jnp.bfloat16, pltpu.SemaphoreType.DMA
    weight = tail_weight.reshape(cols, LANES)

    def wide(*shape):
        return pltpu.VMEM(shape, f32)

    lt3, panel = pl.pallas_call(
        gather,
        name="gather",
        out_shape=(
            jax.ShapeDtypeStruct((group, factors // group, nobl), bf16),
            jax.ShapeDtypeStruct((factors, nsc), bf16),
        ),
        in_specs=[vmem] * 2,
        out_specs=(vmem, vmem),
        scratch_shapes=[
            pltpu.VMEM((PIECES, scenarios.shape[0], nsc // PIECES), bf16),
            dma((GATHER_SENDS,)), dma((2,)), dma((far_x, PIECES)), dma((group, 2)), dma((PIECES,)),
        ],
        compiler_params=pltpu.CompilerParams(collective_id=0, has_side_effects=True),
    )(loadings.T, scenarios)
    loss, cont = pl.pallas_call(
        scenario_losses,
        name="scenario_losses",
        out_shape=(
            jax.ShapeDtypeStruct((cols + TILE, LANES), f32),
            jax.ShapeDtypeStruct((rows, LANES), f32),
        ),
        in_specs=[pl.BlockSpec(memory_space=pltpu.SMEM)] + [vmem] * 6,
        out_specs=(vmem, vmem),
        scratch_shapes=[
            pltpu.VMEM((factors, nobl), bf16),
            pltpu.VMEM((nsc, factors), bf16),
            wide(nsc, LANES), wide(nsc, LANES), wide(8, nobl),
            wide(rows, LANES), wide(rows, LANES), wide(rows, LANES), wide(rows, LANES),
            wide(ROWS, COLS), wide(ROWS, COLS),
        ],
    )(
        thresholds, lt3, panel, rho.reshape(rows, LANES), exposure.reshape(rows, LANES),
        rating.reshape(rows, LANES), weight,
    )
    losses, contributions, shortfall = pl.pallas_call(
        reduce,
        name="reduce",
        out_shape=(
            jax.ShapeDtypeStruct((cols, LANES), f32),
            jax.ShapeDtypeStruct((rows, LANES), f32),
            jax.ShapeDtypeStruct((TILE, LANES), f32),
        ),
        in_specs=[vmem] * 3,
        out_specs=(vmem, vmem, vmem),
        scratch_shapes=[
            wide(cols + TILE, LANES), wide(X, cols + TILE, LANES),
            wide(rows, LANES), wide(Z, rows, LANES), wide(Y, rows, LANES), wide(group, TILE, LANES),
            dma((REDUCE_SENDS,)), dma((2,)), dma((X,)), dma((Z,)), dma((Y,)), dma((group,)),
        ],
        compiler_params=pltpu.CompilerParams(collective_id=1, has_side_effects=True),
    )(loss, cont, weight)
    losses, contributions, shortfall = pl.pallas_call(
        functools.partial(finish, count),
        name="finish",
        out_shape=(
            jax.ShapeDtypeStruct((cols, LANES), f32),
            jax.ShapeDtypeStruct((rows, LANES), f32),
            jax.ShapeDtypeStruct((1, 1), f32),
        ),
        in_specs=[vmem] * 3,
        out_specs=(vmem, vmem, pl.BlockSpec(memory_space=pltpu.SMEM)),
    )(losses, contributions, shortfall)
    return losses.reshape(-1), contributions.reshape(-1), shortfall.reshape(())


def solution(mesh):
    placed = (P("obl", "scen"), P("obl", "scen"), P("obl"), P("obl"), P("obl"), P(), P("scen"))
    return jax.shard_map(
        local, mesh=mesh, in_specs=placed, out_specs=(P("scen"), P("obl"), P()), check_vma=False
    )
```
